32 devices in a mesh: comp: 2 (over core), space: 8 (over z, x), trc: 2 (over y).
Axes of the slice: x: 2, y: 2, z: 4, core: 2. Of those that a mesh axis runs over, the one named last changes fastest.
Arguments:
- tracers: float32 [16, 8, 64, 1024], P(('comp', 'trc'), None, 'space'), may hold values from -6 to 6
- flow: float32 [16, 64, 1024], P(('comp', 'trc'), 'space'), may hold values from -4 to 4
- reaction_rates: float32 [16, 16], replicated, may hold values from -1.5 to 1.5
- land_mask: int32 [64, 1024], P('space'), may hold values 0 or 1
- layers: int32 [64, 1024], P('space'), may hold values from 1 to 8
Outputs:
- tracers_out: float32 [16, 8, 64, 1024], P(('comp', 'trc'), None, 'space')
- flow_out: float32 [16, 64, 1024], P(('comp', 'trc'), 'space')
The draws below stay inside these ranges and needn't reach their ends.
All inputs are finite; a program needn't handle non-finite values. No bound on the sum of `land_mask` on one device may be relied on, other than what follows from the above.
Results may differ from the reference program's by a relative error of at most 0.0003.
Values sent between devices are 32-bit elements; how exact they have to be, the bound alone decides.
No kernel may reach another device: no remote copies, remote signals or barrier semaphores. Data moves between devices by JAX's collectives and lax.ppermute only.
A program may use at most 64 MiB of HBM per device.

```python
import jax
import jax.numpy as jnp
from jax import lax

NTR = 16
NZ = 8
STEPS = 2
NY = 1024
NX = 64


def place_ends(drawn, own_key, low, top_value):
    place = [jax.random.randint(jax.random.fold_in(own_key, axis), (), 0, length) for axis, length in enumerate(drawn.shape)]
    longest = drawn.shape.index(max(drawn.shape))
    next_to = place[:longest] + [(place[longest] + 1) % drawn.shape[longest]] + place[longest + 1:]
    return drawn.at[tuple(place)].set(low).at[tuple(next_to)].set(top_value)


def level_of(own_key, dims, shards, least, top_value):
    def one(dim, blocks):
        heights = jax.random.uniform(jax.random.fold_in(jax.random.fold_in(own_key, 6), dim), (blocks,), jnp.float32, least / len(shards), top_value / len(shards))
        return jnp.repeat(jnp.exp(heights), dims[dim] // blocks).reshape((-1,) + (1,) * (len(dims) - dim - 1))

    factor_of = one(*shards[0])
    for cut in shards[1:]:
        factor_of = factor_of * one(*cut)
    return factor_of


def gaussian(key, shape, scale, reach, shards=(), kind=jnp.bfloat16):
    array = jax.random.normal(key, shape, jnp.float32) * scale
    if len(shards) > 0:
        array = level_of(key, shape, shards, -0.22, 0.18) * array
    return jnp.clip(array, min=-reach, max=reach).astype(kind)


def setup_inputs(seed: int = 0) -> dict:
    splits = jax.random.split(jax.random.key(seed), 6)
    return {
        "tracers": gaussian(splits[0], (NTR, NZ, NX, NY), 1.0, 6.0, ((0, 4), (2, 8)), jnp.float32),
        "flow": gaussian(splits[1], (2 * NZ, NX, NY), 1.0, 4.0, ((0, 4), (1, 8)), jnp.float32),
        "reaction_rates": gaussian(splits[2], (NTR, NTR), NTR ** -0.5, 1.5, (), jnp.float32),
        "land_mask": place_ends((jax.random.randint(splits[3], (NX, NY), 0, 5) < 4).astype(jnp.int32), jax.random.fold_in(splits[3], 1), 0, 1),
        "layers": place_ends(jax.random.randint(splits[4], (NX, NY), 1, NZ + 1), jax.random.fold_in(splits[4], 1), 1, NZ).astype(jnp.int32),
    }


courant = 0.25
viscosity = 0.2
coriolis = 0.3
friction = 0.1
diffusion = 0.3
react_step = 0.5


def trimmed(values, front, back, along):
    along = along % values.ndim
    return lax.slice_in_dim(values, front, values.shape[along] - back, axis=along)


def padded(values, width, along):
    along = along % values.ndim
    spec = [(0, 0)] * values.ndim
    spec[along] = (width, width)
    return jnp.pad(values, spec)


def minmod(first, second):
    return 0.5 * (jnp.sign(first) + jnp.sign(second)) * jnp.minimum(jnp.abs(first), jnp.abs(second))


def sweep(field, speed, wetness, along):
    jumps = trimmed(field, 1, 0, along) - trimmed(field, 0, 1, along)
    slopes = minmod(trimmed(jumps, 0, 1, along), trimmed(jumps, 1, 0, along))
    faces = 0.5 * (trimmed(speed, 0, 1, along) + trimmed(speed, 1, 0, along)) * trimmed(wetness, 0, 1, along) * trimmed(wetness, 1, 0, along)
    upper = jnp.maximum(faces, 0.0)
    lower = jnp.minimum(faces, 0.0)
    fluxes = upper * (trimmed(field, 1, 2, along) + 0.5 * (1.0 - courant * upper) * trimmed(slopes, 0, 1, along)) + lower * (trimmed(field, 2, 1, along) - 0.5 * (1.0 + courant * lower) * trimmed(slopes, 1, 0, along))
    return -courant * (trimmed(fluxes, 1, 0, along) - trimmed(fluxes, 0, 1, along))


def tendency(field, east, north, wetness):
    across = sweep(field, east, wetness, -2)
    inner = trimmed(field, 2, 2, -2)
    north_in = trimmed(north, 1, 1, -2)
    wet_in = trimmed(wetness, 1, 1, -2)
    return across + sweep(padded(inner, 2, -1), padded(north_in, 1, -1), padded(wet_in, 1, -1), -1)


def mixing(field, wetness):
    flows = diffusion * trimmed(wetness, 1, 0, -3) * trimmed(wetness, 0, 1, -3) * (trimmed(field, 1, 0, -3) - trimmed(field, 0, 1, -3))
    edged = padded(flows, 1, -3)
    return field + (trimmed(edged, 1, 0, -3) - trimmed(edged, 0, 1, -3))


def laplace(ghosted):
    widened = padded(ghosted, 1, -1)
    center = widened[:, 1:-1, 1:-1]
    return widened[:, 2:, 1:-1] + widened[:, :-2, 1:-1] + widened[:, 1:-1, 2:] + widened[:, 1:-1, :-2] - 4.0 * center


def react(field, rates):
    flat = field.reshape(field.shape[0], -1)
    soft = flat / (1.0 + jnp.abs(flat))
    return field + react_step * jnp.dot(rates, soft, precision=lax.Precision.HIGHEST).reshape(field.shape)


def wet_cells(land_mask, layers, depth):
    levels = lax.broadcasted_iota(jnp.int32, (depth,) + land_mask.shape, 0)
    return jnp.where((levels < layers[None]) & (land_mask[None] > 0), 1.0, 0.0).astype(jnp.float32)


def reference(tracers, flow, reaction_rates, land_mask, layers):
    wetness = wet_cells(land_mask, layers, NZ)
    wet_pad = padded(wetness, 1, -2)
    east_flow = flow[:NZ]
    north_flow = flow[NZ:]
    for step_index in range(STEPS):
        east_new = wetness * (east_flow + coriolis * north_flow + viscosity * laplace(padded(east_flow, 1, -2)) - friction * east_flow)
        north_new = wetness * (north_flow + (-coriolis) * east_flow + viscosity * laplace(padded(north_flow, 1, -2)) - friction * north_flow)
        east_flow = east_new
        north_flow = north_new
        east_pad = padded(east_flow, 1, -2)
        north_pad = padded(north_flow, 1, -2)

        def advance(column):
            first = column + tendency(padded(column, 2, -2), east_pad, north_pad, wet_pad)
            second = 0.5 * ((column + first) + tendency(padded(first, 2, -2), east_pad, north_pad, wet_pad))
            return mixing(second, wetness)

        tracers = lax.map(advance, tracers)
        tracers = react(tracers, reaction_rates)
    return tracers, jnp.concatenate([east_flow, north_flow], 0)
```

```python
import functools

import jax
import jax.numpy as jnp
from jax import lax
from jax.experimental import pallas as pl
from jax.experimental.pallas import tpu as pltpu
from jax.sharding import Mesh, PartitionSpec as P

STEPS = 2
LANES = 128
ROWS = 8
HALO = 8

courant = 0.25
viscosity = 0.2
coriolis = 0.3
friction = 0.1
diffusion = 0.3
react_step = 0.5

GROUP = ("sx", "comp", "trc")


def minmod(a, b):
    return jnp.maximum(jnp.minimum(a, b), 0.0) + jnp.minimum(jnp.maximum(a, b), 0.0)


def layout(cells, levels):
    flow = cells * ROWS
    depth = flow + levels * ROWS
    edge = depth + ROWS
    size = edge + -(-(cells + levels + 1) // 8) * 8
    return flow, depth, edge, size


def pack_kernel(cells, levels, blocks, t_ref, f_ref, m_ref, l_ref, o_ref, d_ref):
    flow, depth, edge, size = layout(cells, levels)
    d_ref[...] = jnp.where(m_ref[...] > 0, l_ref[...], 0).astype(jnp.float32)
    lane = lax.broadcasted_iota(jnp.int32, (size - edge, LANES), 1)
    filler = size - edge - cells - levels - 1

    def rows(x, block):
        parts = [
            o_ref[block, pl.ds(x, cells, stride=ROWS), :],
            o_ref[block, pl.ds(flow + x, levels, stride=ROWS), :],
            o_ref[block, pl.ds(depth + x, 1), :],
        ]
        if filler:
            parts.append(jnp.zeros((filler, LANES), jnp.float32))
        return jnp.concatenate(parts, axis=0)

    for block in range(blocks):
        cols = pl.ds(block * LANES, LANES)
        o_ref[block, pl.ds(0, flow), :] = t_ref[:, cols]
        o_ref[block, pl.ds(flow, depth - flow), :] = f_ref[:, cols]
        o_ref[block, pl.ds(depth, ROWS), :] = d_ref[:, cols]
    for block in range(blocks):
        packed = jnp.zeros((size - edge, LANES), jnp.float32)
        for x in range(ROWS):
            zeros = jnp.zeros((size - edge, LANES), jnp.float32)
            left = rows(x, block - 1) if block > 0 else zeros
            right = rows(x, block + 1) if block < blocks - 1 else zeros
            both = jnp.where(lane >= LANES - HALO, left, right)
            moved = pltpu.roll(both, (2 * HALO * x + HALO) % LANES, 1)
            packed = jnp.where(lane // (2 * HALO) == x, moved, packed)
        o_ref[block, pl.ds(edge, size - edge), :] = packed


def unpack_kernel(cells, levels, blocks, p_ref, t_ref, f_ref):
    flow = cells * ROWS
    for block in range(blocks):
        cols = pl.ds(block * LANES, LANES)
        t_ref[:, cols] = p_ref[block, pl.ds(0, flow), :]
        f_ref[:, cols] = p_ref[block, pl.ds(flow, levels * ROWS), :]


def main_kernel(
    cells, levels, depth_levels, groups,
    own_ref, low_ref, high_ref, rates_ref, out_ref,
    c_ref, d_ref, u_ref, v_ref, wet_ref, u1_ref, v1_ref, fx_ref, gx_ref, fy_ref, gy_ref,
):
    flow, depth, edge, size = layout(cells, levels)
    wide = LANES + 2 * HALO
    nz = depth_levels
    ntr = LANES // nz
    total = 4 * ROWS

    def spread(load, put, load_edges):
        for x in range(ROWS):
            put(x, HALO, load(x).T)
        turned = load_edges().T
        for x in range(ROWS):
            put(x, 0, turned[2 * HALO * x : 2 * HALO * x + HALO])
            put(x, HALO + LANES, turned[2 * HALO * x + HALO : 2 * HALO * (x + 1)])

    half = groups // 2

    def segment(ref, first, base):
        def put_to(target):
            def put(x, start, value):
                target[base + x, pl.ds(start, value.shape[0]), :] = value
            return put

        spread(
            lambda x: jnp.concatenate(
                [ref[first + g, pl.ds(x, cells, stride=ROWS), :] for g in range(groups)], axis=0
            ),
            put_to(c_ref),
            lambda: jnp.concatenate(
                [ref[first + g, pl.ds(edge, cells), :] for g in range(groups)], axis=0
            ),
        )
        for part, target in ((0, u_ref), (1, v_ref)):
            def whole(value):
                return jnp.concatenate([value] * ntr, axis=0)

            spread(
                lambda x: whole(jnp.concatenate(
                    [ref[first + part * half + g, pl.ds(flow + x, levels, stride=ROWS), :]
                     for g in range(half)], axis=0)),
                put_to(target),
                lambda: whole(jnp.concatenate(
                    [ref[first + part * half + g, pl.ds(edge + cells, levels), :]
                     for g in range(half)], axis=0)),
            )

        def put_wet(x, start, value):
            level = lax.broadcasted_iota(jnp.int32, value.shape, 1) % nz
            wet_ref[base + x, pl.ds(start, value.shape[0]), :] = jnp.where(
                level.astype(jnp.float32) < value, 1.0, 0.0
            )

        def whole_row(value):
            return jnp.broadcast_to(value, (LANES, LANES))

        spread(
            lambda x: whole_row(ref[first, pl.ds(depth + x, 1), :]),
            put_wet,
            lambda: whole_row(ref[first, pl.ds(edge + cells + levels, 1), :]),
        )

    segment(low_ref, 0, 0)
    segment(own_ref, 0, ROWS)
    segment(own_ref, groups, 2 * ROWS)
    segment(high_ref, 0, 3 * ROWS)

    def up(value):
        return pltpu.roll(value, wide - 1, 0)

    def down(value):
        return pltpu.roll(value, 1, 0)

    level = lax.broadcasted_iota(jnp.int32, (wide, LANES), 1) % nz
    inner = jnp.where(level < nz - 1, diffusion, 0.0)

    row_s = lax.broadcasted_iota(jnp.int32, (LANES, ntr), 0) // nz
    pick = jnp.where(row_s == lax.broadcasted_iota(jnp.int32, (LANES, ntr), 1), 1.0, 0.0)
    same = (
        lax.broadcasted_iota(jnp.int32, (LANES, LANES), 0) % nz
        == lax.broadcasted_iota(jnp.int32, (LANES, LANES), 1) % nz
    )
    high = lax.Precision.HIGHEST
    wide_rates = jnp.dot(jnp.dot(pick, rates_ref[...].T, precision=high), pick.T, precision=high)
    mixer = jnp.where(same, react_step * wide_rates, 0.0)

    def slope(a, b, c):
        return minmod(b - a, c - b)

    def flux(f, g, a, b, sa, sb):
        ahead = f > 0.0
        return f * jnp.where(ahead, a, b) + g * jnp.where(ahead, sa, sb)

    def tendency(src, first, last, finish):
        a0, b0, c0 = src[first - 2], src[first - 1], src[first]
        d0 = src[first + 1]
        s_b = slope(a0, b0, c0)
        s_c = slope(b0, c0, d0)
        fl = flux(fx_ref[first - 1], gx_ref[first - 1], b0, c0, s_b, s_c)

        def body(x, carry):
            s_x, fl_x = carry
            row, after, far = src[x], src[x + 1], src[x + 2]
            s_n = slope(row, after, far)
            fl_n = flux(fx_ref[x], gx_ref[x], row, after, s_x, s_n)
            right = up(row)
            jump = right - row
            s_y = minmod(down(jump), jump)
            fl_y = flux(fy_ref[x], gy_ref[x], row, right, s_y, up(s_y))
            finish(x, row, (fl_x - fl_n) + (down(fl_y) - fl_y))
            return s_n, fl_n

        lax.fori_loop(first, last, body, (s_c, fl))

    us, vs = (u_ref, u1_ref), (v_ref, v1_ref)
    for step in range(STEPS):
        margin = 4 * step
        u_old, u_new = us[step % 2], us[1 - step % 2]
        v_old, v_new = vs[step % 2], vs[1 - step % 2]

        def velocity(x, _):
            wet = wet_ref[x]
            u, v = u_old[x], v_old[x]
            lap_u = u_old[x - 1] + u_old[x + 1] + up(u) + down(u) - 4.0 * u
            lap_v = v_old[x - 1] + v_old[x + 1] + up(v) + down(v) - 4.0 * v
            u_new[x] = wet * (u + coriolis * v + viscosity * lap_u - friction * u)
            v_new[x] = wet * (v - coriolis * u + viscosity * lap_v - friction * v)
            return 0

        lax.fori_loop(margin + 1, total - 1 - margin, velocity, 0)

        def faces(x, _):
            wet = wet_ref[x]
            fx = (0.5 * courant) * (u_new[x] + u_new[x + 1]) * (wet * wet_ref[x + 1])
            v = v_new[x]
            fy = (0.5 * courant) * (v + up(v)) * (wet * up(wet))
            fx_ref[x], fy_ref[x] = fx, fy
            ax, ay = jnp.abs(fx), jnp.abs(fy)
            gx_ref[x] = 0.5 * ax * (1.0 - ax)
            gy_ref[x] = 0.5 * ay * (1.0 - ay)
            return 0

        lax.fori_loop(margin + 1, total - 2 - margin, faces, 0)

        def first_stage(x, row, change):
            d_ref[x] = row + change

        tendency(c_ref, margin + 2, total - 2 - margin, first_stage)

        def second_stage(x, row, change):
            second = 0.5 * ((c_ref[x] + row) + change)
            wet = wet_ref[x]
            below = pltpu.roll(second, LANES - 1, 1)
            g = inner * (wet * pltpu.roll(wet, LANES - 1, 1)) * (below - second)
            mixed = second + (g - pltpu.roll(g, 1, 1))
            soft = mixed / (1.0 + jnp.abs(mixed))
            c_ref[x] = mixed + jnp.dot(soft, mixer, precision=high)

        tendency(d_ref, margin + 4, total - 4 - margin, second_stage)

    u_last, v_last = us[STEPS % 2], vs[STEPS % 2]
    lane = lax.broadcasted_iota(jnp.int32, (LANES, LANES), 1)
    for part in range(2):
        for x in range(ROWS):
            row = (1 + part) * ROWS + x
            turned = c_ref[row, pl.ds(HALO, LANES), :].T
            moves = jnp.where(
                lane < nz, u_last[row, pl.ds(HALO, LANES), :], v_last[row, pl.ds(HALO, LANES), :]
            ).T
            for g in range(groups):
                out_ref[part * groups + g, pl.ds(x, cells, stride=ROWS), :] = turned[
                    cells * g : cells * (g + 1)
                ]
                out_ref[part * groups + g, pl.ds(flow + x, levels, stride=ROWS), :] = moves[
                    levels * g : levels * (g + 1)
                ]


def params():
    return pltpu.CompilerParams(vmem_limit_bytes=60 * 1024 * 1024)


def body(tracers, flow, reaction_rates, land_mask, layers):
    species, nz, rows, ny = tracers.shape
    levels = flow.shape[0]
    cells = species * nz
    groups = lax.axis_size("comp") * lax.axis_size("trc")
    blocks = 2 * groups
    assert rows == ROWS and ny == blocks * LANES and groups * cells == LANES
    _, _, _, size = layout(cells, levels)
    f32 = jnp.float32
    vmem = pl.BlockSpec(memory_space=pltpu.VMEM)

    packed = pl.pallas_call(
        functools.partial(pack_kernel, cells, levels, blocks),
        out_shape=jax.ShapeDtypeStruct((blocks, size, LANES), f32),
        in_specs=[vmem] * 4,
        out_specs=vmem,
        scratch_shapes=[pltpu.VMEM((ROWS, ny), f32)],
        compiler_params=params(),
        name="pack",
    )(tracers.reshape(cells * rows, ny), flow.reshape(levels * rows, ny), land_mask, layers)
    own = lax.all_to_all(packed, GROUP, 0, 0, tiled=True)
    count = lax.axis_size("sz")
    forward = [(i, i + 1) for i in range(count - 1)]
    backward = [(i + 1, i) for i in range(count - 1)]
    low = lax.ppermute(own[groups:], "sz", forward)
    high = lax.ppermute(own[:groups], "sz", backward)

    wide = LANES + 2 * HALO
    field = pltpu.VMEM((4 * ROWS, wide, LANES), f32)
    out = pl.pallas_call(
        functools.partial(main_kernel, cells, levels, nz, groups),
        out_shape=jax.ShapeDtypeStruct((blocks, (cells + levels) * ROWS, LANES), f32),
        in_specs=[vmem] * 4,
        out_specs=vmem,
        scratch_shapes=[field] * 11,
        compiler_params=params(),
        name="advance",
    )(own, low, high, reaction_rates)
    back = lax.all_to_all(out, GROUP, 0, 0, tiled=True)
    new_tracers, new_flow = pl.pallas_call(
        functools.partial(unpack_kernel, cells, levels, blocks),
        out_shape=(
            jax.ShapeDtypeStruct((cells * rows, ny), f32),
            jax.ShapeDtypeStruct((levels * rows, ny), f32),
        ),
        in_specs=[vmem],
        out_specs=(vmem, vmem),
        compiler_params=params(),
        name="unpack",
    )(back)
    return new_tracers.reshape(tracers.shape), new_flow.reshape(flow.shape)


def solution(mesh):
    comp, space, trc = (mesh.shape[name] for name in ("comp", "space", "trc"))
    finer = Mesh(
        mesh.devices.reshape(comp, space // 2, 2, trc), ("comp", "sz", "sx", "trc")
    )
    strips = ("sz", "sx")
    placed = (
        P(("comp", "trc"), None, strips, None),
        P(("comp", "trc"), strips, None),
        P(),
        P(strips, None),
        P(strips, None),
    )
    return jax.shard_map(
        body,
        mesh=finer,
        in_specs=placed,
        out_specs=(P(("comp", "trc"), None, strips, None), P(("comp", "trc"), strips, None)),
        check_vma=False,
    )
```

```python
import functools

import jax
import jax.numpy as jnp
from jax import lax
from jax.experimental import pallas as pl
from jax.experimental.pallas import tpu as pltpu
from jax.sharding import Mesh, PartitionSpec as P

STEPS = 2
LANES = 128
ROWS = 8
HALO = 8

courant = 0.25
viscosity = 0.2
coriolis = 0.3
friction = 0.1
diffusion = 0.3
react_step = 0.5

GROUP = ("sx", "comp", "trc")


def minmod(a, b):
    return jnp.maximum(jnp.minimum(a, b), 0.0) + jnp.minimum(jnp.maximum(a, b), 0.0)


def layout(cells, levels):
    flow = cells * ROWS
    depth = flow + levels * ROWS
    edge = depth + ROWS
    size = edge + -(-(cells + levels + 1) // 8) * 8
    return flow, depth, edge, size


def group_index():
    sx, comp, trc = (lax.axis_index(name) for name in GROUP)
    inner = lax.axis_size("trc")
    return (sx * lax.axis_size("comp") + comp) * inner + trc


def pack_kernel(cells, levels, blocks, t_ref, f_ref, m_ref, l_ref, *refs):
    outs, (o_ref, d_ref) = refs[:blocks], refs[blocks:]
    flow, depth, edge, size = layout(cells, levels)
    d_ref[...] = jnp.where(m_ref[...] > 0, l_ref[...], 0).astype(jnp.float32)
    lane = lax.broadcasted_iota(jnp.int32, (size - edge, LANES), 1)
    filler = size - edge - cells - levels - 1
    own = group_index()

    def rows(x, block):
        parts = [
            o_ref[block, pl.ds(x, cells, stride=ROWS), :],
            o_ref[block, pl.ds(flow + x, levels, stride=ROWS), :],
            o_ref[block, pl.ds(depth + x, 1), :],
        ]
        if filler:
            parts.append(jnp.zeros((filler, LANES), jnp.float32))
        return jnp.concatenate(parts, axis=0)

    for block in range(blocks):
        cols = pl.ds(block * LANES, LANES)
        o_ref[block, pl.ds(0, flow), :] = t_ref[:, cols]
        o_ref[block, pl.ds(flow, depth - flow), :] = f_ref[:, cols]
        o_ref[block, pl.ds(depth, ROWS), :] = d_ref[:, cols]
    for block in range(blocks):
        packed = jnp.zeros((size - edge, LANES), jnp.float32)
        for x in range(ROWS):
            zeros = jnp.zeros((size - edge, LANES), jnp.float32)
            left = rows(x, block - 1) if block > 0 else zeros
            right = rows(x, block + 1) if block < blocks - 1 else zeros
            both = jnp.where(lane >= LANES - HALO, left, right)
            moved = pltpu.roll(both, (2 * HALO * x + HALO) % LANES, 1)
            packed = jnp.where(lane // (2 * HALO) == x, moved, packed)
        o_ref[block, pl.ds(edge, size - edge), :] = packed
    for way in range(blocks):
        outs[way][...] = o_ref[jnp.bitwise_xor(own, way)]


def unpack_kernel(cells, levels, blocks, *refs):
    ins, (t_ref, f_ref) = refs[:blocks], refs[blocks:]
    flow = cells * ROWS
    own = group_index()
    for way in range(blocks):
        start = jnp.bitwise_xor(own, way) * LANES
        cols = pl.ds(pl.multiple_of(start, LANES), LANES)
        t_ref[:, cols] = ins[way][pl.ds(0, flow), :]
        f_ref[:, cols] = ins[way][pl.ds(flow, levels * ROWS), :]


def sorted_by(parts, own):
    bit = 1
    while bit < len(parts):
        swap = jnp.bitwise_and(own, bit) > 0
        parts = [jnp.where(swap, parts[i ^ bit], parts[i]) for i in range(len(parts))]
        bit *= 2
    return parts


def main_kernel(cells, levels, depth_levels, groups, *refs):
    blocks = 2 * groups
    own_refs, far_refs = refs[:blocks], refs[blocks : 2 * blocks]
    rates_ref = refs[2 * blocks]
    out_refs = refs[2 * blocks + 1 : 3 * blocks + 1]
    c_ref, d_ref, u_ref, v_ref, wet_ref, u1_ref, v1_ref, fx_ref, gx_ref, fy_ref, gy_ref = refs[
        3 * blocks + 1 :
    ]
    flow, depth, edge, size = layout(cells, levels)
    wide = LANES + 2 * HALO
    nz = depth_levels
    ntr = LANES // nz
    total = 4 * ROWS
    half = groups // 2
    sx = lax.axis_index("sx")
    own = jnp.bitwise_and(group_index(), groups - 1)

    def spread(load, put, load_edges):
        for x in range(ROWS):
            put(x, HALO, load(x).T)
        turned = load_edges().T
        for x in range(ROWS):
            put(x, 0, turned[2 * HALO * x : 2 * HALO * x + HALO])
            put(x, HALO + LANES, turned[2 * HALO * x + HALO : 2 * HALO * (x + 1)])

    def segment(parts, base):
        def put_to(target):
            def put(x, start, value):
                target[base + x, pl.ds(start, value.shape[0]), :] = value
            return put

        spread(
            lambda x: jnp.concatenate(
                [ref[pl.ds(x, cells, stride=ROWS), :] for ref in parts], axis=0
            ),
            put_to(c_ref),
            lambda: jnp.concatenate([ref[pl.ds(edge, cells), :] for ref in parts], axis=0),
        )

        def component(which, place, **step):
            pieces = sorted_by([ref[pl.ds(place, levels, **step), :] for ref in parts], own)
            return jnp.concatenate(pieces[which * half : (which + 1) * half] * ntr, axis=0)

        for which, target in ((0, u_ref), (1, v_ref)):
            spread(
                lambda x: component(which, flow + x, stride=ROWS),
                put_to(target),
                lambda: component(which, edge + cells),
            )

        def put_wet(x, start, value):
            level = lax.broadcasted_iota(jnp.int32, value.shape, 1) % nz
            wet_ref[base + x, pl.ds(start, value.shape[0]), :] = jnp.where(
                level.astype(jnp.float32) < value, 1.0, 0.0
            )

        def whole_row(value):
            return jnp.broadcast_to(value, (LANES, LANES))

        spread(
            lambda x: whole_row(parts[0][pl.ds(depth + x, 1), :]),
            put_wet,
            lambda: whole_row(parts[0][pl.ds(edge + cells + levels, 1), :]),
        )

    segment(own_refs[:groups], ROWS + ROWS * sx)
    segment(own_refs[groups:], 2 * ROWS - ROWS * sx)
    segment(far_refs[:groups], 3 * ROWS * (1 - sx))
    segment(far_refs[groups:], 3 * ROWS * sx)

    def up(value):
        return pltpu.roll(value, wide - 1, 0)

    def down(value):
        return pltpu.roll(value, 1, 0)

    level = lax.broadcasted_iota(jnp.int32, (wide, LANES), 1) % nz
    inner = jnp.where(level < nz - 1, diffusion, 0.0)

    lane_of = lax.broadcasted_iota(jnp.int32, (LANES, ntr), 0)
    holder = jnp.bitwise_xor(lane_of // cells, own)
    row_s = (holder * cells + lane_of % cells) // nz
    pick = jnp.where(row_s == lax.broadcasted_iota(jnp.int32, (LANES, ntr), 1), 1.0, 0.0)
    same = (
        lax.broadcasted_iota(jnp.int32, (LANES, LANES), 0) % nz
        == lax.broadcasted_iota(jnp.int32, (LANES, LANES), 1) % nz
    )
    high = lax.Precision.HIGHEST
    wide_rates = jnp.dot(jnp.dot(pick, rates_ref[...].T, precision=high), pick.T, precision=high)
    mixer = jnp.where(same, react_step * wide_rates, 0.0)

    def slope(a, b, c):
        return minmod(b - a, c - b)

    def flux(f, g, a, b, sa, sb):
        ahead = f > 0.0
        return f * jnp.where(ahead, a, b) + g * jnp.where(ahead, sa, sb)

    def tendency(src, first, last, finish):
        a0, b0, c0 = src[first - 2], src[first - 1], src[first]
        d0 = src[first + 1]
        s_b = slope(a0, b0, c0)
        s_c = slope(b0, c0, d0)
        fl = flux(fx_ref[first - 1], gx_ref[first - 1], b0, c0, s_b, s_c)

        def body(x, carry):
            s_x, fl_x = carry
            row, after, far = src[x], src[x + 1], src[x + 2]
            s_n = slope(row, after, far)
            fl_n = flux(fx_ref[x], gx_ref[x], row, after, s_x, s_n)
            right = up(row)
            jump = right - row
            s_y = minmod(down(jump), jump)
            fl_y = flux(fy_ref[x], gy_ref[x], row, right, s_y, up(s_y))
            finish(x, row, (fl_x - fl_n) + (down(fl_y) - fl_y))
            return s_n, fl_n

        lax.fori_loop(first, last, body, (s_c, fl))

    us, vs = (u_ref, u1_ref), (v_ref, v1_ref)
    for step in range(STEPS):
        margin = 4 * step
        u_old, u_new = us[step % 2], us[1 - step % 2]
        v_old, v_new = vs[step % 2], vs[1 - step % 2]

        def velocity(x, _):
            wet = wet_ref[x]
            u, v = u_old[x], v_old[x]
            lap_u = u_old[x - 1] + u_old[x + 1] + up(u) + down(u) - 4.0 * u
            lap_v = v_old[x - 1] + v_old[x + 1] + up(v) + down(v) - 4.0 * v
            u_new[x] = wet * (u + coriolis * v + viscosity * lap_u - friction * u)
            v_new[x] = wet * (v - coriolis * u + viscosity * lap_v - friction * v)
            return 0

        lax.fori_loop(margin + 1, total - 1 - margin, velocity, 0)

        def faces(x, _):
            wet = wet_ref[x]
            fx = (0.5 * courant) * (u_new[x] + u_new[x + 1]) * (wet * wet_ref[x + 1])
            v = v_new[x]
            fy = (0.5 * courant) * (v + up(v)) * (wet * up(wet))
            fx_ref[x], fy_ref[x] = fx, fy
            ax, ay = jnp.abs(fx), jnp.abs(fy)
            gx_ref[x] = 0.5 * ax * (1.0 - ax)
            gy_ref[x] = 0.5 * ay * (1.0 - ay)
            return 0

        lax.fori_loop(margin + 1, total - 2 - margin, faces, 0)

        def first_stage(x, row, change):
            d_ref[x] = row + change

        tendency(c_ref, margin + 2, total - 2 - margin, first_stage)

        def second_stage(x, row, change):
            second = 0.5 * ((c_ref[x] + row) + change)
            wet = wet_ref[x]
            below = pltpu.roll(second, LANES - 1, 1)
            g = inner * (wet * pltpu.roll(wet, LANES - 1, 1)) * (below - second)
            mixed = second + (g - pltpu.roll(g, 1, 1))
            soft = mixed / (1.0 + jnp.abs(mixed))
            c_ref[x] = mixed + jnp.dot(soft, mixer, precision=high)

        tendency(d_ref, margin + 4, total - 4 - margin, second_stage)

    u_last, v_last = us[STEPS % 2], vs[STEPS % 2]
    lane = lax.broadcasted_iota(jnp.int32, (LANES, LANES), 1)
    for part in range(2):
        base = ROWS + ROWS * sx if part == 0 else 2 * ROWS - ROWS * sx
        for x in range(ROWS):
            row = base + x
            turned = c_ref[row, pl.ds(HALO, LANES), :].T
            moves = jnp.where(
                lane < nz, u_last[row, pl.ds(HALO, LANES), :], v_last[row, pl.ds(HALO, LANES), :]
            ).T
            moves = sorted_by([moves[levels * g : levels * (g + 1)] for g in range(groups)], own)
            for g in range(groups):
                ref = out_refs[part * groups + g]
                ref[pl.ds(x, cells, stride=ROWS), :] = turned[cells * g : cells * (g + 1)]
                ref[pl.ds(flow + x, levels, stride=ROWS), :] = moves[g]


def params(mib):
    return pltpu.CompilerParams(vmem_limit_bytes=mib * 1024 * 1024)


def body(tracers, flow, reaction_rates, land_mask, layers):
    species, nz, rows, ny = tracers.shape
    levels = flow.shape[0]
    cells = species * nz
    groups = lax.axis_size("comp") * lax.axis_size("trc")
    blocks = 2 * groups
    assert rows == ROWS and ny == blocks * LANES and groups * cells == LANES
    _, _, _, size = layout(cells, levels)
    f32 = jnp.float32
    vmem = pl.BlockSpec(memory_space=pltpu.VMEM)

    packed = pl.pallas_call(
        functools.partial(pack_kernel, cells, levels, blocks),
        out_shape=[jax.ShapeDtypeStruct((size, LANES), f32)] * blocks,
        in_specs=[vmem] * 4,
        out_specs=[vmem] * blocks,
        scratch_shapes=[pltpu.VMEM((blocks, size, LANES), f32), pltpu.VMEM((ROWS, ny), f32)],
        compiler_params=params(8),
        name="pack",
    )(tracers.reshape(cells * rows, ny), flow.reshape(levels * rows, ny), land_mask, layers)

    def exchange(pieces):
        inner = lax.axis_size("trc")

        def placed(member):
            strip, rest = divmod(member, groups)
            core, chip = divmod(rest, inner)
            return (core * 2 + strip) * inner + chip

        return [
            piece if way == 0
            else lax.ppermute(
                piece, ("comp", "sx", "trc"), [(placed(i), placed(i ^ way)) for i in range(blocks)]
            )
            for way, piece in enumerate(pieces)
        ]

    own = exchange(packed)
    count = lax.axis_size("sz")
    near = [(2 * z + 1, 2 * z + 3) for z in range(count - 1)]
    near += [(2 * z + 2, 2 * z) for z in range(count - 1)]
    away = [(2 * z, 2 * z + 2) for z in range(count - 1)]
    away += [(2 * z + 3, 2 * z + 1) for z in range(count - 1)]
    far = [
        lax.ppermute(piece, ("sz", "sx"), near if way < groups else away)
        for way, piece in enumerate(own)
    ]

    wide = LANES + 2 * HALO
    field = pltpu.VMEM((4 * ROWS, wide, LANES), f32)
    out = pl.pallas_call(
        functools.partial(main_kernel, cells, levels, nz, groups),
        out_shape=[jax.ShapeDtypeStruct(((cells + levels) * ROWS, LANES), f32)] * blocks,
        in_specs=[vmem] * (2 * blocks + 1),
        out_specs=[vmem] * blocks,
        scratch_shapes=[field] * 11,
        compiler_params=params(40),
        name="advance",
    )(*own, *far, reaction_rates)
    new_tracers, new_flow = pl.pallas_call(
        functools.partial(unpack_kernel, cells, levels, blocks),
        out_shape=(
            jax.ShapeDtypeStruct((cells * rows, ny), f32),
            jax.ShapeDtypeStruct((levels * rows, ny), f32),
        ),
        in_specs=[vmem] * blocks,
        out_specs=(vmem, vmem),
        compiler_params=params(8),
        name="unpack",
    )(*exchange(out))
    return new_tracers.reshape(tracers.shape), new_flow.reshape(flow.shape)


def solution(mesh):
    comp, space, trc = (mesh.shape[name] for name in ("comp", "space", "trc"))
    finer = Mesh(
        mesh.devices.reshape(comp, space // 2, 2, trc), ("comp", "sz", "sx", "trc")
    )
    strips = ("sz", "sx")
    placed = (
        P(("comp", "trc"), None, strips, None),
        P(("comp", "trc"), strips, None),
        P(),
        P(strips, None),
        P(strips, None),
    )
    return jax.shard_map(
        body,
        mesh=finer,
        in_specs=placed,
        out_specs=(P(("comp", "trc"), None, strips, None), P(("comp", "trc"), strips, None)),
        check_vma=False,
    )
```

```python
import functools

import jax
import jax.numpy as jnp
from jax import lax
from jax.experimental import pallas as pl
from jax.experimental.pallas import tpu as pltpu
from jax.sharding import Mesh, PartitionSpec as P

STEPS = 2
LANES = 128
ROWS = 8
HALO = 8

courant = 0.25
viscosity = 0.2
coriolis = 0.3
friction = 0.1
diffusion = 0.3
react_step = 0.5

GROUP = ("sx", "comp", "trc")


def minmod(a, b):
    return jnp.maximum(jnp.minimum(a, b), 0.0) + jnp.minimum(jnp.maximum(a, b), 0.0)


def layout(cells, levels):
    flow = cells * ROWS
    depth = flow + levels * ROWS
    edge = depth + ROWS
    size = edge + -(-(cells + levels + 1) // 8) * 8
    return flow, depth, edge, size


def group_index():
    sx, comp, trc = (lax.axis_index(name) for name in GROUP)
    inner = lax.axis_size("trc")
    return (sx * lax.axis_size("comp") + comp) * inner + trc


def pack_kernel(cells, levels, blocks, t_ref, f_ref, m_ref, l_ref, *refs):
    outs, (o_ref, d_ref) = refs[:blocks], refs[blocks:]
    flow, depth, edge, size = layout(cells, levels)
    d_ref[...] = jnp.where(m_ref[...] > 0, l_ref[...], 0).astype(jnp.float32)
    lane = lax.broadcasted_iota(jnp.int32, (size - edge, LANES), 1)
    filler = size - edge - cells - levels - 1
    own = group_index()

    def rows(x, block):
        parts = [
            o_ref[block, pl.ds(x, cells, stride=ROWS), :],
            o_ref[block, pl.ds(flow + x, levels, stride=ROWS), :],
            o_ref[block, pl.ds(depth + x, 1), :],
        ]
        if filler:
            parts.append(jnp.zeros((filler, LANES), jnp.float32))
        return jnp.concatenate(parts, axis=0)

    for block in range(blocks):
        cols = pl.ds(block * LANES, LANES)
        o_ref[block, pl.ds(0, flow), :] = t_ref[:, cols]
        o_ref[block, pl.ds(flow, depth - flow), :] = f_ref[:, cols]
        o_ref[block, pl.ds(depth, ROWS), :] = d_ref[:, cols]
    for block in range(blocks):
        packed = jnp.zeros((size - edge, LANES), jnp.float32)
        for x in range(ROWS):
            zeros = jnp.zeros((size - edge, LANES), jnp.float32)
            left = rows(x, block - 1) if block > 0 else zeros
            right = rows(x, block + 1) if block < blocks - 1 else zeros
            both = jnp.where(lane >= LANES - HALO, left, right)
            moved = pltpu.roll(both, (2 * HALO * x + HALO) % LANES, 1)
            packed = jnp.where(lane // (2 * HALO) == x, moved, packed)
        o_ref[block, pl.ds(edge, size - edge), :] = packed
    for way in range(blocks):
        outs[way][...] = o_ref[jnp.bitwise_xor(own, way)]


def unpack_kernel(cells, levels, blocks, *refs):
    ins, (t_ref, f_ref) = refs[:blocks], refs[blocks:]
    flow = cells * ROWS
    own = group_index()
    for way in range(blocks):
        start = jnp.bitwise_xor(own, way) * LANES
        cols = pl.ds(pl.multiple_of(start, LANES), LANES)
        t_ref[:, cols] = ins[way][pl.ds(0, flow), :]
        f_ref[:, cols] = ins[way][pl.ds(flow, levels * ROWS), :]


def sorted_by(parts, own):
    bit = 1
    while bit < len(parts):
        swap = jnp.bitwise_and(own, bit) > 0
        parts = [jnp.where(swap, parts[i ^ bit], parts[i]) for i in range(len(parts))]
        bit *= 2
    return parts


def main_kernel(cells, levels, depth_levels, groups, *refs):
    blocks = 2 * groups
    own_refs, far_refs = refs[:blocks], refs[blocks : 2 * blocks]
    rates_ref = refs[2 * blocks]
    out_refs = refs[2 * blocks + 1 : 3 * blocks + 1]
    c_ref, d_ref, u_ref, u1_ref, dep_ref, weight_ref, open_ref, f_ref, g_ref, mixer_ref = refs[
        3 * blocks + 1 :
    ]
    flow, depth, edge, size = layout(cells, levels)
    wide = LANES + 2 * HALO
    nz = depth_levels
    ntr = LANES // nz
    total = 4 * ROWS
    sx = lax.axis_index("sx")
    own = jnp.bitwise_and(group_index(), groups - 1)

    def spread(load, put, load_edges):
        for x in range(ROWS):
            put(x, HALO, load(x).T)
        turned = load_edges().T
        for x in range(ROWS):
            put(x, 0, turned[2 * HALO * x : 2 * HALO * x + HALO])
            put(x, HALO + LANES, turned[2 * HALO * x + HALO : 2 * HALO * (x + 1)])

    lane = lax.broadcasted_iota(jnp.int32, (wide, LANES), 1)
    level = lane % nz
    second_part = lane % (2 * nz) >= nz

    def segment(parts, place):
        base = place * ROWS

        def put(x, start, value):
            c_ref[base + x, pl.ds(start, value.shape[0]), :] = value

        spread(
            lambda x: jnp.concatenate(
                [ref[pl.ds(x, cells, stride=ROWS), :] for ref in parts], axis=0
            ),
            put,
            lambda: jnp.concatenate([ref[pl.ds(edge, cells), :] for ref in parts], axis=0),
        )

        def flows(start, **step):
            pieces = [ref[pl.ds(start, levels, **step), :] for ref in parts]
            return sorted_by(pieces, own)

        rows = sum((flows(flow + x, stride=ROWS) for x in range(ROWS)), [])
        u_ref[place, pl.ds(HALO, LANES), :] = jnp.concatenate(rows, axis=0).T
        ends = jnp.concatenate(flows(edge + cells) * ROWS, axis=0).T

        deep = parts[0]
        rows = [
            jnp.broadcast_to(deep[pl.ds(depth + x, 1), :], (2 * nz, LANES)) for x in range(ROWS)
        ]
        dep_ref[place, pl.ds(HALO, LANES), :] = jnp.concatenate(rows, axis=0).T
        deep_ends = jnp.broadcast_to(
            deep[pl.ds(edge + cells + levels, 1), :], (LANES, LANES)
        ).T
        slot = lax.broadcasted_iota(jnp.int32, (HALO, LANES), 1) // (2 * nz)
        for side in range(2):
            for source, target in ((ends, u_ref), (deep_ends, dep_ref)):
                value = source[side * HALO : (side + 1) * HALO]
                for x in range(1, ROWS):
                    first = (2 * x + side) * HALO
                    value = jnp.where(slot == x, source[first : first + HALO], value)
                target[place, pl.ds(side * (HALO + LANES), HALO), :] = value

    segment(own_refs[:groups], 1 + sx)
    segment(own_refs[groups:], 2 - sx)
    segment(far_refs[:groups], 3 * (1 - sx))
    segment(far_refs[groups:], 3 * sx)

    def up(value):
        return pltpu.roll(value, wide - 1, 0)

    def down(value):
        return pltpu.roll(value, 1, 0)

    strips = total // ROWS
    stride = 2 * nz

    def next_row(ref, place):
        follow = min(place + 1, strips - 1)
        shift = LANES - stride
        return jnp.where(
            lane < LANES - stride, pltpu.roll(ref[place], shift, 1), pltpu.roll(ref[follow], shift, 1)
        )

    def prior_row(ref, place):
        before = max(place - 1, 0)
        return jnp.where(
            lane >= stride, pltpu.roll(ref[place], stride, 1), pltpu.roll(ref[before], stride, 1)
        )

    def wetness(value):
        return jnp.where(level.astype(jnp.float32) < value, 1.0, 0.0)

    for place in range(strips):
        value = dep_ref[place]
        wet = wetness(value)
        weight_ref[place] = jnp.where(
            level.astype(jnp.float32) + 1.0 < jnp.minimum(value, float(nz)), diffusion, 0.0
        )
        along = jnp.where(second_part, up(wet), wetness(next_row(dep_ref, place)))
        open_ref[place] = (0.5 * courant) * (wet * along)

    lane_of = lax.broadcasted_iota(jnp.int32, (LANES, ntr), 0)
    holder = jnp.bitwise_xor(lane_of // cells, own)
    row_s = (holder * cells + lane_of % cells) // nz
    pick = jnp.where(row_s == lax.broadcasted_iota(jnp.int32, (LANES, ntr), 1), 1.0, 0.0)
    same = (
        lax.broadcasted_iota(jnp.int32, (LANES, LANES), 0) % nz
        == lax.broadcasted_iota(jnp.int32, (LANES, LANES), 1) % nz
    )
    high = lax.Precision.HIGHEST
    wide_rates = jnp.dot(jnp.dot(pick, rates_ref[...].T, precision=high), pick.T, precision=high)
    mixer = jnp.where(same, react_step * wide_rates, 0.0)
    coarse = mixer.astype(jnp.bfloat16)
    fine = (mixer - coarse.astype(jnp.float32)).astype(jnp.bfloat16)
    mixer_ref[...] = jnp.concatenate(
        [
            jnp.concatenate([coarse, fine], axis=1),
            jnp.concatenate([coarse, jnp.zeros_like(fine)], axis=1),
        ],
        axis=0,
    )

    def gathered(ref, x, part):
        index = level + (stride * jnp.bitwise_and(x, ROWS - 1) + part * nz)
        return jnp.take_along_axis(ref[lax.shift_right_logical(x, 3)], index, axis=1)

    def slope(a, b, c):
        return minmod(b - a, c - b)

    def flux(f, g, a, b, sa, sb):
        ahead = f > 0.0
        return f * jnp.where(ahead, a, b) + g * jnp.where(ahead, sa, sb)

    def tendency(src, first, last, finish):
        a0, b0, c0 = src[first - 2], src[first - 1], src[first]
        d0 = src[first + 1]
        s_b = slope(a0, b0, c0)
        s_c = slope(b0, c0, d0)
        start = jnp.int32(first - 1)
        fl = flux(gathered(f_ref, start, 0), gathered(g_ref, start, 0), b0, c0, s_b, s_c)

        def body(x, carry):
            s_x, fl_x = carry
            row, after, far = src[x], src[x + 1], src[x + 2]
            s_n = slope(row, after, far)
            fl_n = flux(gathered(f_ref, x, 0), gathered(g_ref, x, 0), row, after, s_x, s_n)
            right = up(row)
            jump = right - row
            s_y = minmod(down(jump), jump)
            fl_y = flux(gathered(f_ref, x, 1), gathered(g_ref, x, 1), row, right, s_y, up(s_y))
            finish(x, row, (fl_x - fl_n) + (down(fl_y) - fl_y))
            return s_n, fl_n

        lax.fori_loop(first, last, body, (s_c, fl))

    fields = (u_ref, u1_ref)
    turn = jnp.where(second_part, -coriolis, coriolis)
    for step in range(STEPS):
        margin = 4 * step
        old, new = fields[step % 2], fields[1 - step % 2]
        for place in range(strips):
            u = old[place]
            other = jnp.where(second_part, pltpu.roll(u, nz, 1), pltpu.roll(u, LANES - nz, 1))
            lap = prior_row(old, place) + next_row(old, place) + up(u) + down(u) - 4.0 * u
            new[place] = wetness(dep_ref[place]) * (
                u + turn * other + viscosity * lap - friction * u
            )
        for place in range(strips):
            u = new[place]
            f = (u + jnp.where(second_part, up(u), next_row(new, place))) * open_ref[place]
            size_f = jnp.abs(f)
            f_ref[place] = f
            g_ref[place] = 0.5 * size_f * (1.0 - size_f)

        def first_stage(x, row, change):
            d_ref[x] = row + change

        tendency(c_ref, margin + 2, total - 2 - margin, first_stage)

        def second_stage(x, row, change):
            c_ref[x] = 0.5 * ((c_ref[x] + row) + change)

        tendency(d_ref, margin + 4, total - 4 - margin, second_stage)

        def react(x, _):
            second = c_ref[x]
            below = pltpu.roll(second, LANES - 1, 1)
            g = gathered(weight_ref, x, 0) * (below - second)
            mixed = second + (g - pltpu.roll(g, 1, 1))
            soft = mixed / (1.0 + jnp.abs(mixed))
            coarse = soft.astype(jnp.bfloat16)
            fine = (soft - coarse.astype(jnp.float32)).astype(jnp.bfloat16)
            sums = jnp.dot(
                jnp.concatenate([coarse, fine], axis=1), mixer_ref[...],
                preferred_element_type=jnp.float32,
            )
            c_ref[x] = mixed + (sums[:, :LANES] + sums[:, LANES:])
            return 0

        lax.fori_loop(margin + 4, total - 4 - margin, react, 0)

    last_field = fields[STEPS % 2]
    for part in range(2):
        place = 1 + sx if part == 0 else 2 - sx
        moves = last_field[place, pl.ds(HALO, LANES), :].T
        for x in range(ROWS):
            turned = c_ref[place * ROWS + x, pl.ds(HALO, LANES), :].T
            first = x * stride
            pieces = sorted_by(
                [moves[first + levels * g : first + levels * (g + 1)] for g in range(groups)], own
            )
            for g in range(groups):
                ref = out_refs[part * groups + g]
                ref[pl.ds(x, cells, stride=ROWS), :] = turned[cells * g : cells * (g + 1)]
                ref[pl.ds(flow + x, levels, stride=ROWS), :] = pieces[g]


def params(mib):
    return pltpu.CompilerParams(vmem_limit_bytes=mib * 1024 * 1024)


def body(tracers, flow, reaction_rates, land_mask, layers):
    species, nz, rows, ny = tracers.shape
    levels = flow.shape[0]
    cells = species * nz
    groups = lax.axis_size("comp") * lax.axis_size("trc")
    blocks = 2 * groups
    assert rows == ROWS and ny == blocks * LANES and groups * cells == LANES
    _, _, _, size = layout(cells, levels)
    f32 = jnp.float32
    vmem = pl.BlockSpec(memory_space=pltpu.VMEM)

    packed = pl.pallas_call(
        functools.partial(pack_kernel, cells, levels, blocks),
        out_shape=[jax.ShapeDtypeStruct((size, LANES), f32)] * blocks,
        in_specs=[vmem] * 4,
        out_specs=[vmem] * blocks,
        scratch_shapes=[pltpu.VMEM((blocks, size, LANES), f32), pltpu.VMEM((ROWS, ny), f32)],
        compiler_params=params(8),
        name="pack",
    )(tracers.reshape(cells * rows, ny), flow.reshape(levels * rows, ny), land_mask, layers)

    def exchange(pieces):
        inner = lax.axis_size("trc")

        def placed(member):
            strip, rest = divmod(member, groups)
            core, chip = divmod(rest, inner)
            return (core * 2 + strip) * inner + chip

        return [
            piece if way == 0
            else lax.ppermute(
                piece, ("comp", "sx", "trc"), [(placed(i), placed(i ^ way)) for i in range(blocks)]
            )
            for way, piece in enumerate(pieces)
        ]

    own = exchange(packed)
    count = lax.axis_size("sz")
    near = [(2 * z + 1, 2 * z + 3) for z in range(count - 1)]
    near += [(2 * z + 2, 2 * z) for z in range(count - 1)]
    away = [(2 * z, 2 * z + 2) for z in range(count - 1)]
    away += [(2 * z + 3, 2 * z + 1) for z in range(count - 1)]
    far = [
        lax.ppermute(piece, ("sz", "sx"), near if way < groups else away)
        for way, piece in enumerate(own)
    ]

    wide = LANES + 2 * HALO
    field = pltpu.VMEM((4 * ROWS, wide, LANES), f32)
    compact = pltpu.VMEM((4, wide, LANES), f32)
    out = pl.pallas_call(
        functools.partial(main_kernel, cells, levels, nz, groups),
        out_shape=[jax.ShapeDtypeStruct(((cells + levels) * ROWS, LANES), f32)] * blocks,
        in_specs=[vmem] * (2 * blocks + 1),
        out_specs=[vmem] * blocks,
        scratch_shapes=[field] * 2 + [compact] * 7 + [pltpu.VMEM((2 * LANES, 2 * LANES), jnp.bfloat16)],
        compiler_params=params(40),
        name="advance",
    )(*own, *far, reaction_rates)
    new_tracers, new_flow = pl.pallas_call(
        functools.partial(unpack_kernel, cells, levels, blocks),
        out_shape=(
            jax.ShapeDtypeStruct((cells * rows, ny), f32),
            jax.ShapeDtypeStruct((levels * rows, ny), f32),
        ),
        in_specs=[vmem] * blocks,
        out_specs=(vmem, vmem),
        compiler_params=params(8),
        name="unpack",
    )(*exchange(out))
    return new_tracers.reshape(tracers.shape), new_flow.reshape(flow.shape)


def solution(mesh):
    comp, space, trc = (mesh.shape[name] for name in ("comp", "space", "trc"))
    finer = Mesh(
        mesh.devices.reshape(comp, space // 2, 2, trc), ("comp", "sz", "sx", "trc")
    )
    strips = ("sz", "sx")
    placed = (
        P(("comp", "trc"), None, strips, None),
        P(("comp", "trc"), strips, None),
        P(),
        P(strips, None),
        P(strips, None),
    )
    return jax.shard_map(
        body,
        mesh=finer,
        in_specs=placed,
        out_specs=(P(("comp", "trc"), None, strips, None), P(("comp", "trc"), strips, None)),
        check_vma=False,
    )
```

```python
import functools

import jax
import jax.numpy as jnp
from jax import lax
from jax.experimental import pallas as pl
from jax.experimental.pallas import tpu as pltpu
from jax.sharding import Mesh, PartitionSpec as P

STEPS = 2
LANES = 128
ROWS = 8
HALO = 8
TOGETHER = 8
WEIGH = 4
FACES = 4
SWEEP = 2

courant = 0.25
viscosity = 0.2
coriolis = 0.3
friction = 0.1
diffusion = 0.3
react_step = 0.5

GROUP = ("sx", "comp", "trc")


def minmod(a, b):
    return jnp.maximum(jnp.minimum(a, b), 0.0) + jnp.minimum(jnp.maximum(a, b), 0.0)


def layout(cells, levels):
    flow = cells * ROWS
    depth = flow + levels * ROWS
    edge = depth + ROWS
    size = edge + -(-(cells + levels + 1) // 8) * 8
    return flow, depth, edge, size


def group_index():
    sx, comp, trc = (lax.axis_index(name) for name in GROUP)
    inner = lax.axis_size("trc")
    return (sx * lax.axis_size("comp") + comp) * inner + trc


def pack_kernel(cells, levels, blocks, t_ref, f_ref, m_ref, l_ref, *refs):
    outs, (o_ref, d_ref) = refs[:blocks], refs[blocks:]
    flow, depth, edge, size = layout(cells, levels)
    d_ref[...] = jnp.where(m_ref[...] > 0, l_ref[...], 0).astype(jnp.float32)
    lane = lax.broadcasted_iota(jnp.int32, (size - edge, LANES), 1)
    filler = size - edge - cells - levels - 1
    own = group_index()

    def rows(x, block):
        parts = [
            o_ref[block, pl.ds(x, cells, stride=ROWS), :],
            o_ref[block, pl.ds(flow + x, levels, stride=ROWS), :],
            o_ref[block, pl.ds(depth + x, 1), :],
        ]
        if filler:
            parts.append(jnp.zeros((filler, LANES), jnp.float32))
        return jnp.concatenate(parts, axis=0)

    for block in range(blocks):
        cols = pl.ds(block * LANES, LANES)
        o_ref[block, pl.ds(0, flow), :] = t_ref[:, cols]
        o_ref[block, pl.ds(flow, depth - flow), :] = f_ref[:, cols]
        o_ref[block, pl.ds(depth, ROWS), :] = d_ref[:, cols]
    for block in range(blocks):
        packed = jnp.zeros((size - edge, LANES), jnp.float32)
        for x in range(ROWS):
            zeros = jnp.zeros((size - edge, LANES), jnp.float32)
            left = rows(x, block - 1) if block > 0 else zeros
            right = rows(x, block + 1) if block < blocks - 1 else zeros
            both = jnp.where(lane >= LANES - HALO, left, right)
            moved = pltpu.roll(both, (2 * HALO * x + HALO) % LANES, 1)
            packed = jnp.where(lane // (2 * HALO) == x, moved, packed)
        o_ref[block, pl.ds(edge, size - edge), :] = packed
    for way in range(blocks):
        outs[way][...] = o_ref[jnp.bitwise_xor(own, way)]


def unpack_kernel(cells, levels, blocks, *refs):
    ins, (t_ref, f_ref) = refs[:blocks], refs[blocks:]
    flow = cells * ROWS
    own = group_index()
    for way in range(blocks):
        start = jnp.bitwise_xor(own, way) * LANES
        cols = pl.ds(pl.multiple_of(start, LANES), LANES)
        t_ref[:, cols] = ins[way][pl.ds(0, flow), :]
        f_ref[:, cols] = ins[way][pl.ds(flow, levels * ROWS), :]


def sorted_by(parts, own):
    bit = 1
    while bit < len(parts):
        swap = jnp.bitwise_and(own, bit) > 0
        parts = [jnp.where(swap, parts[i ^ bit], parts[i]) for i in range(len(parts))]
        bit *= 2
    return parts


def main_kernel(cells, levels, depth_levels, groups, *refs):
    blocks = 2 * groups
    own_refs, far_refs = refs[:blocks], refs[blocks : 2 * blocks]
    rates_ref = refs[2 * blocks]
    out_refs = refs[2 * blocks + 1 : 3 * blocks + 1]
    c_ref, d_ref, w_ref, fx_ref, fy_ref, gx_ref, gy_ref = refs[3 * blocks + 1 : 3 * blocks + 8]
    u_ref, u1_ref, dep_ref, weight_ref, open_ref, f_ref, turned_ref, mixer_ref = refs[
        3 * blocks + 8 :
    ]
    flow, depth, edge, size = layout(cells, levels)
    wide = LANES + 2 * HALO
    nz = depth_levels
    ntr = LANES // nz
    total = 4 * ROWS
    sx = lax.axis_index("sx")
    own = jnp.bitwise_and(group_index(), groups - 1)

    def spread(load, put, load_edges):
        for x in range(ROWS):
            put(x, HALO, load(x).T)
        turned = load_edges().T
        for x in range(ROWS):
            put(x, 0, turned[2 * HALO * x : 2 * HALO * x + HALO])
            put(x, HALO + LANES, turned[2 * HALO * x + HALO : 2 * HALO * (x + 1)])

    lane = lax.broadcasted_iota(jnp.int32, (wide, LANES), 1)
    level = lane % nz
    second_part = lane % (2 * nz) >= nz

    def segment(parts, place):
        base = place * ROWS

        def put(x, start, value):
            c_ref[base + x, pl.ds(start, value.shape[0]), :] = value

        spread(
            lambda x: jnp.concatenate(
                [ref[pl.ds(x, cells, stride=ROWS), :] for ref in parts], axis=0
            ),
            put,
            lambda: jnp.concatenate([ref[pl.ds(edge, cells), :] for ref in parts], axis=0),
        )

        def flows(start, **step):
            pieces = [ref[pl.ds(start, levels, **step), :] for ref in parts]
            return sorted_by(pieces, own)

        rows = sum((flows(flow + x, stride=ROWS) for x in range(ROWS)), [])
        u_ref[place, pl.ds(HALO, LANES), :] = jnp.concatenate(rows, axis=0).T
        ends = jnp.concatenate(flows(edge + cells) * ROWS, axis=0).T

        deep = parts[0]
        rows = [
            jnp.broadcast_to(deep[pl.ds(depth + x, 1), :], (2 * nz, LANES)) for x in range(ROWS)
        ]
        dep_ref[place, pl.ds(HALO, LANES), :] = jnp.concatenate(rows, axis=0).T
        deep_ends = jnp.broadcast_to(
            deep[pl.ds(edge + cells + levels, 1), :], (LANES, LANES)
        ).T
        slot = lax.broadcasted_iota(jnp.int32, (HALO, LANES), 1) // (2 * nz)
        for side in range(2):
            for source, target in ((ends, u_ref), (deep_ends, dep_ref)):
                value = source[side * HALO : (side + 1) * HALO]
                for x in range(1, ROWS):
                    first = (2 * x + side) * HALO
                    value = jnp.where(slot == x, source[first : first + HALO], value)
                target[place, pl.ds(side * (HALO + LANES), HALO), :] = value

    segment(own_refs[:groups], 1 + sx)
    segment(own_refs[groups:], 2 - sx)
    segment(far_refs[:groups], 3 * (1 - sx))
    segment(far_refs[groups:], 3 * sx)

    def up(value):
        return pltpu.roll(value, wide - 1, 0)

    def down(value):
        return pltpu.roll(value, 1, 0)

    strips = total // ROWS
    stride = 2 * nz

    def next_row(ref, place):
        follow = min(place + 1, strips - 1)
        shift = LANES - stride
        return jnp.where(
            lane < LANES - stride, pltpu.roll(ref[place], shift, 1), pltpu.roll(ref[follow], shift, 1)
        )

    def prior_row(ref, place):
        before = max(place - 1, 0)
        return jnp.where(
            lane >= stride, pltpu.roll(ref[place], stride, 1), pltpu.roll(ref[before], stride, 1)
        )

    def wetness(value):
        return jnp.where(level.astype(jnp.float32) < value, 1.0, 0.0)

    for place in range(strips):
        value = dep_ref[place]
        wet = wetness(value)
        weight_ref[place] = jnp.where(
            level.astype(jnp.float32) + 1.0 < jnp.minimum(value, float(nz)), diffusion, 0.0
        )
        along = jnp.where(second_part, up(wet), wetness(next_row(dep_ref, place)))
        open_ref[place] = (0.5 * courant) * (wet * along)

    lane_of = lax.broadcasted_iota(jnp.int32, (LANES, ntr), 0)
    holder = jnp.bitwise_xor(lane_of // cells, own)
    row_s = (holder * cells + lane_of % cells) // nz
    pick = jnp.where(row_s == lax.broadcasted_iota(jnp.int32, (LANES, ntr), 1), 1.0, 0.0)
    same = (
        lax.broadcasted_iota(jnp.int32, (LANES, LANES), 0) % nz
        == lax.broadcasted_iota(jnp.int32, (LANES, LANES), 1) % nz
    )
    high = lax.Precision.HIGHEST
    wide_rates = jnp.dot(jnp.dot(pick, rates_ref[...].T, precision=high), pick.T, precision=high)
    mixer = jnp.where(same, react_step * wide_rates, 0.0)
    coarse = mixer.astype(jnp.bfloat16)
    fine = (mixer - coarse.astype(jnp.float32)).astype(jnp.bfloat16)
    mixer_ref[...] = jnp.concatenate(
        [
            jnp.concatenate([coarse, fine], axis=1),
            jnp.concatenate([coarse, jnp.zeros_like(fine)], axis=1),
        ],
        axis=0,
    )

    def turn_over(ref):
        for place in range(strips):
            turned_ref[place] = ref[place, pl.ds(HALO, LANES), :].T

    ends = lax.broadcasted_iota(jnp.int32, (2 * HALO, LANES), 1) % nz

    def spread_out(ref, x, part, put):
        place = lax.shift_right_logical(x, 3)
        first = stride * jnp.bitwise_and(x, ROWS - 1) + part * nz
        level_rows = turned_ref[place, pl.ds(pl.multiple_of(first, nz), nz), :]
        put(HALO, jnp.concatenate([level_rows] * ntr, axis=0).T)
        outer = jnp.concatenate(
            [ref[place, pl.ds(0, HALO), :], ref[place, pl.ds(HALO + LANES, HALO), :]], axis=0
        )
        outer = jnp.take_along_axis(outer, ends + first, axis=1)
        put(0, outer[:HALO])
        put(HALO + LANES, outer[HALO:])

    def each(first, last, run, together):
        turns, rest = divmod(last - first, together)

        def turn_of(i, _):
            for k in range(together):
                run(first + together * i + k)
            return 0

        lax.fori_loop(0, turns, turn_of, 0)
        for k in range(rest):
            run(jnp.int32(last - rest + k))

    turn_over(weight_ref)

    def weigh(x):
        def put(start, value):
            w_ref[x, pl.ds(start, value.shape[0]), :] = value
        spread_out(weight_ref, x, 0, put)

    each(4, total - 4, weigh, WEIGH)

    def slope(a, b, c):
        return minmod(b - a, c - b)

    def flux(f, g, a, b, sa, sb):
        ahead = f > 0.0
        return f * jnp.where(ahead, a, b) + g * jnp.where(ahead, sa, sb)

    def tendency(src, first, last, finish):
        a0, b0, c0 = src[first - 2], src[first - 1], src[first]
        d0 = src[first + 1]
        s_b = slope(a0, b0, c0)
        s_c = slope(b0, c0, d0)
        fl = flux(fx_ref[first - 1], gx_ref[first - 1], b0, c0, s_b, s_c)

        def body(x, carry):
            s_x, fl_x = carry
            row, after, far = src[x], src[x + 1], src[x + 2]
            s_n = slope(row, after, far)
            fl_n = flux(fx_ref[x], gx_ref[x], row, after, s_x, s_n)
            right = up(row)
            jump = right - row
            s_y = minmod(down(jump), jump)
            fl_y = flux(fy_ref[x], gy_ref[x], row, right, s_y, up(s_y))
            finish(x, row, (fl_x - fl_n) + (down(fl_y) - fl_y))
            return s_n, fl_n

        def turn_of(i, carry):
            for k in range(SWEEP):
                carry = body(first + SWEEP * i + k, carry)
            return carry

        lax.fori_loop(0, (last - first) // SWEEP, turn_of, (s_c, fl))

    fields = (u_ref, u1_ref)
    turn = jnp.where(second_part, -coriolis, coriolis)
    for step in range(STEPS):
        margin = 4 * step
        old, new = fields[step % 2], fields[1 - step % 2]
        for place in range(strips):
            u = old[place]
            other = jnp.where(second_part, pltpu.roll(u, nz, 1), pltpu.roll(u, LANES - nz, 1))
            lap = prior_row(old, place) + next_row(old, place) + up(u) + down(u) - 4.0 * u
            new[place] = wetness(dep_ref[place]) * (
                u + turn * other + viscosity * lap - friction * u
            )
        for place in range(strips):
            u = new[place]
            f_ref[place] = (
                u + jnp.where(second_part, up(u), next_row(new, place))
            ) * open_ref[place]
        turn_over(f_ref)

        def faces(x):
            for part, f_out, g_out in ((0, fx_ref, gx_ref), (1, fy_ref, gy_ref)):
                def put(start, value):
                    where = pl.ds(start, value.shape[0])
                    size_f = jnp.abs(value)
                    f_out[x, where, :] = value
                    g_out[x, where, :] = 0.5 * size_f * (1.0 - size_f)
                spread_out(f_ref, x, part, put)

        each(margin + 1, total - 2 - margin, faces, FACES)

        def first_stage(x, row, change):
            d_ref[x] = row + change

        tendency(c_ref, margin + 2, total - 2 - margin, first_stage)

        def second_stage(x, row, change):
            c_ref[x] = 0.5 * ((c_ref[x] + row) + change)

        tendency(d_ref, margin + 4, total - 4 - margin, second_stage)

        def react(i, _):
            rows = pl.ds(margin + 4 + TOGETHER * i, TOGETHER)
            shape = (TOGETHER * wide, LANES)
            second = c_ref[rows].reshape(shape)
            below = pltpu.roll(second, LANES - 1, 1)
            g = w_ref[rows].reshape(shape) * (below - second)
            mixed = second + (g - pltpu.roll(g, 1, 1))
            soft = mixed / (1.0 + jnp.abs(mixed))
            coarse = soft.astype(jnp.bfloat16)
            fine = (soft - coarse.astype(jnp.float32)).astype(jnp.bfloat16)
            sums = jnp.dot(
                jnp.concatenate([coarse, fine], axis=1), mixer_ref[...],
                preferred_element_type=jnp.float32,
            )
            c_ref[rows] = (mixed + (sums[:, :LANES] + sums[:, LANES:])).reshape(
                TOGETHER, wide, LANES
            )
            return 0

        lax.fori_loop(0, (total - 8 - 2 * margin) // TOGETHER, react, 0)

    last_field = fields[STEPS % 2]
    for part in range(2):
        place = 1 + sx if part == 0 else 2 - sx
        moves = last_field[place, pl.ds(HALO, LANES), :].T
        for x in range(ROWS):
            turned = c_ref[place * ROWS + x, pl.ds(HALO, LANES), :].T
            first = x * stride
            pieces = sorted_by(
                [moves[first + levels * g : first + levels * (g + 1)] for g in range(groups)], own
            )
            for g in range(groups):
                ref = out_refs[part * groups + g]
                ref[pl.ds(x, cells, stride=ROWS), :] = turned[cells * g : cells * (g + 1)]
                ref[pl.ds(flow + x, levels, stride=ROWS), :] = pieces[g]


def params(mib):
    return pltpu.CompilerParams(vmem_limit_bytes=mib * 1024 * 1024)


def body(tracers, flow, reaction_rates, land_mask, layers):
    species, nz, rows, ny = tracers.shape
    levels = flow.shape[0]
    cells = species * nz
    groups = lax.axis_size("comp") * lax.axis_size("trc")
    blocks = 2 * groups
    assert rows == ROWS and ny == blocks * LANES and groups * cells == LANES
    _, _, _, size = layout(cells, levels)
    f32 = jnp.float32
    vmem = pl.BlockSpec(memory_space=pltpu.VMEM)

    packed = pl.pallas_call(
        functools.partial(pack_kernel, cells, levels, blocks),
        out_shape=[jax.ShapeDtypeStruct((size, LANES), f32)] * blocks,
        in_specs=[vmem] * 4,
        out_specs=[vmem] * blocks,
        scratch_shapes=[pltpu.VMEM((blocks, size, LANES), f32), pltpu.VMEM((ROWS, ny), f32)],
        compiler_params=params(8),
        name="pack",
    )(tracers.reshape(cells * rows, ny), flow.reshape(levels * rows, ny), land_mask, layers)

    def exchange(pieces):
        inner = lax.axis_size("trc")

        def placed(member):
            strip, rest = divmod(member, groups)
            core, chip = divmod(rest, inner)
            return (core * 2 + strip) * inner + chip

        return [
            piece if way == 0
            else lax.ppermute(
                piece, ("comp", "sx", "trc"), [(placed(i), placed(i ^ way)) for i in range(blocks)]
            )
            for way, piece in enumerate(pieces)
        ]

    own = exchange(packed)
    count = lax.axis_size("sz")
    near = [(2 * z + 1, 2 * z + 3) for z in range(count - 1)]
    near += [(2 * z + 2, 2 * z) for z in range(count - 1)]
    away = [(2 * z, 2 * z + 2) for z in range(count - 1)]
    away += [(2 * z + 3, 2 * z + 1) for z in range(count - 1)]
    far = [
        lax.ppermute(piece, ("sz", "sx"), near if way < groups else away)
        for way, piece in enumerate(own)
    ]

    wide = LANES + 2 * HALO
    field = pltpu.VMEM((4 * ROWS, wide, LANES), f32)
    compact = pltpu.VMEM((4, wide, LANES), f32)
    out = pl.pallas_call(
        functools.partial(main_kernel, cells, levels, nz, groups),
        out_shape=[jax.ShapeDtypeStruct(((cells + levels) * ROWS, LANES), f32)] * blocks,
        in_specs=[vmem] * (2 * blocks + 1),
        out_specs=[vmem] * blocks,
        scratch_shapes=[field] * 7
        + [compact] * 6
        + [
            pltpu.VMEM((4, LANES, LANES), f32),
            pltpu.VMEM((2 * LANES, 2 * LANES), jnp.bfloat16),
        ],
        compiler_params=params(40),
        name="advance",
    )(*own, *far, reaction_rates)
    new_tracers, new_flow = pl.pallas_call(
        functools.partial(unpack_kernel, cells, levels, blocks),
        out_shape=(
            jax.ShapeDtypeStruct((cells * rows, ny), f32),
            jax.ShapeDtypeStruct((levels * rows, ny), f32),
        ),
        in_specs=[vmem] * blocks,
        out_specs=(vmem, vmem),
        compiler_params=params(8),
        name="unpack",
    )(*exchange(out))
    return new_tracers.reshape(tracers.shape), new_flow.reshape(flow.shape)


def solution(mesh):
    comp, space, trc = (mesh.shape[name] for name in ("comp", "space", "trc"))
    finer = Mesh(
        mesh.devices.reshape(comp, space // 2, 2, trc), ("comp", "sz", "sx", "trc")
    )
    strips = ("sz", "sx")
    placed = (
        P(("comp", "trc"), None, strips, None),
        P(("comp", "trc"), strips, None),
        P(),
        P(strips, None),
        P(strips, None),
    )
    return jax.shard_map(
        body,
        mesh=finer,
        in_specs=placed,
        out_specs=(P(("comp", "trc"), None, strips, None), P(("comp", "trc"), strips, None)),
        check_vma=False,
    )
```
